32 devices in a mesh: lat: 4 (over y, core), lon: 8 (over z, x).
Axes of the slice: x: 2, y: 2, z: 4, core: 2. Of those that a mesh axis runs over, the one named last changes fastest.
Arguments:
- field: bfloat16 [64, 128, 384], P('lat', 'lon'), may hold values from -6 to 6
- obs_jac: bfloat16 [32, 32, 128, 384], P(None, ('lat', 'lon')), may hold values from -0.3125 to 0.3125
- obs_frac: bfloat16 [32, 32, 2, 128], P(None, ('lat', 'lon')), may hold values from 0 to 1
- obs_innov: bfloat16 [32, 32, 128], P(None, ('lat', 'lon')), may hold values from -6 to 6
- obs_rinv: bfloat16 [32, 32, 128], P(None, ('lat', 'lon')), may hold values from 1 to 16
- obs_cells: int32 [32, 32, 128], P(None, ('lat', 'lon')), may hold values from -1 to 270, as said below
Outputs:
- departures: float32 [32, 32, 128], P(None, ('lat', 'lon'))
- field_grad: float32 [64, 128, 384], P('lat', 'lon')
The draws below stay inside these ranges and needn't reach their ends.
Inputs may be any that keep to these rules, and one draw needn't show every extreme that they name: `obs_cells`: in block (o, p) the live slots come first, at least one and at most 128; a live slot holds r * 17 + q with r below 16 and q below 16; slot 0 of every block holds the cell at r = 15, q = 15; the number of live slots varies by owner.
All inputs are finite; a program needn't handle non-finite values.
Results may differ from the reference program's by a relative error of at most 0.0046.
Values may be sent and summed in bfloat16 or wider, within the bound.
A program may use at most 128 MiB of HBM per device.

```python
import math
import jax
import jax.numpy as jnp
from jax import lax

LAT_DEV = 16
LON_DEV = 16
SLOTS = 128
WIDTH = 384
NLAT = 64
NLON = 128
N_LON = 8
DEVICES = 32


def draw_obs_cells(key, part):
    key_level, key_cut, key_row, key_col, key_pick = jax.random.split(key, 5)
    level_vals = jax.random.randint(key_level, (DEVICES, 1), 1, 5)
    chosen = jax.random.permutation(key_pick, DEVICES)[0]
    level_vals = jnp.where(jnp.arange(DEVICES)[:, None] == chosen, 4, level_vals)
    cut_vals = jax.random.randint(key_cut, (DEVICES, DEVICES), 0, SLOTS // 4)
    live_count = SLOTS * level_vals // 4 - cut_vals
    first_src = jnp.arange(DEVICES)[None, :] == 0
    live_count = jnp.where(first_src & (level_vals == 4), SLOTS, live_count)
    row_vals = jax.random.randint(key_row, (DEVICES, DEVICES, SLOTS), 0, LAT_DEV)
    col_vals = jax.random.randint(key_col, (DEVICES, DEVICES, SLOTS), 0, LON_DEV)
    slot_idx = jnp.arange(SLOTS)[None, None, :]
    cell_vals = row_vals * (LON_DEV + 1) + col_vals
    cell_vals = jnp.where(slot_idx == 0, LAT_DEV * (LON_DEV + 1) - 2, cell_vals)
    cell_vals = jnp.where(slot_idx < live_count[:, :, None], cell_vals, -1)
    return cell_vals.astype(jnp.int32)


def block_levels(own_key, shape, cuts, smallest, largest):
    factor_of = 1.0
    for dim, parts in cuts:
        steps = jax.random.uniform(jax.random.fold_in(jax.random.fold_in(own_key, 6), dim), (parts,), jnp.float32, smallest / len(cuts), largest / len(cuts))
        factor_of = factor_of * jnp.repeat(jnp.exp(steps), shape[dim] // parts).reshape((-1,) + (1,) * (len(shape) - 1 - dim))
    return factor_of


def normal_values(key, shape, scale, reach, cuts=(), kind=jnp.bfloat16):
    values = jax.random.normal(key, shape, jnp.float32) * scale
    if len(cuts) > 0:
        values = block_levels(key, shape, cuts, -0.22, 0.18) * values
    return jnp.clip(values, min=-reach, max=reach).astype(kind)


def setup_inputs(seed: int = 0) -> dict:
    splits = jax.random.split(jax.random.key(seed), 7)
    return {
        "field": normal_values(splits[0], (NLAT, NLON, WIDTH), 1.0, 6.0, ((0, 4), (1, 8))),
        "obs_jac": normal_values(splits[1], (DEVICES, DEVICES, SLOTS, WIDTH), WIDTH ** -0.5, 0.3125, ((1, 32),)),
        "obs_frac": jnp.clip(1.0 * jax.random.uniform(splits[2], (DEVICES, DEVICES, 2, SLOTS), jnp.float32) ** block_levels(splits[2], (DEVICES, DEVICES, 2, SLOTS), ((1, 32),), -0.2, 0.2), 0.0, 1.0).astype(jnp.bfloat16),
        "obs_innov": normal_values(splits[3], (DEVICES, DEVICES, SLOTS), 1.0, 6.0, ((1, 32),)),
        "obs_rinv": jnp.clip(jnp.exp(math.log(16.0) - 2.7725887 * jax.random.uniform(splits[4], (DEVICES, DEVICES, SLOTS), jnp.float32) ** block_levels(splits[4], (DEVICES, DEVICES, SLOTS), ((1, 32),), -0.2, 0.2)), 1.0, 16.0).astype(jnp.bfloat16),
        "obs_cells": draw_obs_cells(jax.random.fold_in(splits[6], 71), 0),
    }


def local_terms(col_table, stride, cell_ids, frac_lat, frac_lon, innovation, inv_error, jacobian, grad_ext):
    is_live = cell_ids >= 0
    corner = jnp.where(is_live, cell_ids, 0).astype(jnp.int32)
    lat_part = frac_lat.astype(jnp.float32)
    lon_part = frac_lon.astype(jnp.float32)
    raw_weights = ((1.0 - lat_part) * (1.0 - lon_part), lat_part * (1.0 - lon_part), (1.0 - lat_part) * lon_part, lat_part * lon_part)
    rounded = lax.optimization_barrier(tuple(weight.astype(jnp.bfloat16) for weight in raw_weights))
    weights = tuple(weight.astype(jnp.float32) for weight in rounded)
    offsets = (0, stride, 1, stride + 1)
    interp = jnp.zeros((cell_ids.shape[0], col_table.shape[1]), jnp.float32)
    for weight, offset in zip(weights, offsets):
        interp = interp + weight[:, None] * col_table[corner + offset].astype(jnp.float32)
    jac_wide = jacobian.astype(jnp.float32)
    evolved = jnp.sum(interp * jac_wide, axis=1)
    departure = jnp.where(is_live, evolved - innovation.astype(jnp.float32), jnp.zeros((), jnp.float32))
    contrib_low = lax.optimization_barrier(((inv_error.astype(jnp.float32) * departure)[:, None] * jac_wide).astype(jnp.bfloat16))
    contrib = contrib_low.astype(jnp.float32)
    for weight, offset in zip(weights, offsets):
        grad_ext = grad_ext.at[corner + offset].add(weight[:, None] * contrib)
    return departure, grad_ext


def reference(field, obs_jac, obs_frac, obs_innov, obs_rinv, obs_cells):
    width_all = field.shape[2]
    stride = LON_DEV + 1
    extended = jnp.concatenate([field, field[:, :1]], axis=1)
    extended = jnp.concatenate([extended, jnp.zeros((1, NLON + 1, width_all), field.dtype)], axis=0)
    owners = jnp.arange(DEVICES, dtype=jnp.int32)

    def visit_owner(grad_all, pieces):
        owner_id, jac_rows, frac_pair, innov_vals, rinv_vals, cell_vals = pieces
        row_start = ((owner_id // N_LON) * LAT_DEV).astype(jnp.int32)
        col_start = ((owner_id % N_LON) * LON_DEV).astype(jnp.int32)
        zero_idx = jnp.zeros((), jnp.int32)
        col_table = lax.dynamic_slice(extended, (row_start, col_start, zero_idx), (LAT_DEV + 1, stride, width_all)).reshape(-1, width_all)
        local_grad = jnp.zeros(((LAT_DEV + 1) * stride, width_all), jnp.float32)
        departure, local_grad = local_terms(col_table, stride, cell_vals.reshape(-1), frac_pair[:, 0, :].reshape(-1), frac_pair[:, 1, :].reshape(-1), innov_vals.reshape(-1), rinv_vals.reshape(-1), jac_rows.reshape(-1, width_all), local_grad)
        old_grad = lax.dynamic_slice(grad_all, (row_start, col_start, zero_idx), (LAT_DEV + 1, stride, width_all))
        grad_all = lax.dynamic_update_slice(grad_all, old_grad + local_grad.reshape(LAT_DEV + 1, stride, width_all), (row_start, col_start, zero_idx))
        return grad_all, departure.reshape(cell_vals.shape)

    grad_all = jnp.zeros((NLAT + 1, NLON + 1, width_all), jnp.float32)
    grad_all, departures = lax.scan(visit_owner, grad_all, (owners, obs_jac, obs_frac, obs_innov, obs_rinv, obs_cells))
    field_grad = grad_all[:NLAT, :NLON].at[:, 0].add(grad_all[:NLAT, NLON])
    return departures, field_grad
```

```python
import functools
import math

import jax
import jax.numpy as jnp
from jax import lax
from jax.experimental import pallas as pl
from jax.experimental.pallas import tpu as pltpu
from jax.sharding import PartitionSpec as P

MESH = pl.DeviceIdType.MESH


def weight_rows(position, frac, rows):
    ids = lax.broadcasted_iota(jnp.int32, (rows, position.shape[1]), 0).astype(jnp.float32)
    zero = jnp.zeros_like(ids)
    return jnp.where(
        ids == position, 1.0 - frac, jnp.where(ids == position + 1.0, frac, zero)
    )


def kernel(
    lat_n, lon_n, line, rows, cols, tile,
    field, edge, meta, jac,
    grad_out, dep_out,
    tbl, met, jrecv, dep, grad, gsend, grecv, hrecv,
    t_send, t_recv, m_send, m_recv, j_send, j_recv, d_send, d_recv,
    g_send, g_recv, h_send, h_recv,
):
    inner = lon_n // line
    plane = lat_n * inner
    total = lat_n * lon_n
    slots = jac.shape[3]
    cells = rows * cols
    lat, lon = lax.axis_index("lat"), lax.axis_index("lon")
    z, xi = lon // inner, lon % inner
    here = lat * inner + xi
    lat_up, lat_down = (lat + 1) % lat_n, (lat + lat_n - 1) % lat_n
    lon_up, lon_down = (lon + 1) % lon_n, (lon + lon_n - 1) % lon_n

    def remote(src, dst, send, recv, to):
        return pltpu.make_async_remote_copy(
            src_ref=src, dst_ref=dst, send_sem=send, recv_sem=recv,
            device_id=to, device_id_type=MESH,
        )

    def landed(dst, sem):
        pltpu.make_async_copy(dst, dst, sem).wait()

    me = lat * lon_n + lon
    barrier = pltpu.get_barrier_semaphore()

    def greet(i, carry):
        other = (me + i) % total
        pl.semaphore_signal(
            barrier, inc=1, device_id=(other // lon_n, other % lon_n), device_id_type=MESH
        )
        return carry

    lax.fori_loop(1, total, greet, 0)

    own_tbl = pltpu.make_async_copy(field, tbl.at[z, pl.ds(0, cells)], t_recv.at[0, z])
    own_tbl.start()
    own_met = pltpu.make_async_copy(
        meta.at[lat, :, xi], met.at[:, :, pl.ds(here * slots, slots)], m_recv.at[here]
    )
    own_met.start()

    def own_jac(g, carry):
        pltpu.make_async_copy(
            jac.at[lat, g, xi], jrecv.at[g, pl.ds(here * slots, slots)], j_recv.at[g, here]
        ).start()
        return carry

    lax.fori_loop(0, line, own_jac, 0)
    pl.semaphore_wait(barrier, total - 1)

    z_low, x_low = lon_down // inner, lon_down % inner
    halo = cells + cols

    def table_copies(i):
        to = (z + i) % line
        return (
            remote(field, tbl.at[z, pl.ds(0, cells)], t_send.at[0, to], t_recv.at[0, z],
                   (lat, to * inner + xi)),
            remote(field.at[pl.ds(0, cols)], tbl.at[z, pl.ds(cells, cols)],
                   t_send.at[1, to], t_recv.at[1, z], (lat_down, to * inner + xi)),
            remote(edge, tbl.at[z_low, pl.ds(halo, rows)], t_send.at[2, to],
                   t_recv.at[2, z_low], (lat, to * inner + x_low)),
            remote(edge, tbl.at[z_low, pl.ds(halo + rows, rows)], t_send.at[3, to],
                   t_recv.at[3, z_low], (lat_down, to * inner + x_low)),
        )

    def meta_copy(i):
        to = (here + i) % plane
        return remote(
            meta.at[to // inner, :, to % inner], met.at[:, :, pl.ds(here * slots, slots)],
            m_send.at[to], m_recv.at[here], (to // inner, z * inner + to % inner),
        )

    def jac_copy(g, i):
        to = (here + i) % plane
        return remote(
            jac.at[to // inner, g, to % inner], jrecv.at[g, pl.ds(here * slots, slots)],
            j_send.at[g, to], j_recv.at[g, here], (to // inner, z * inner + to % inner),
        )

    def dep_copy(g, i):
        to = (here + i) % plane
        return remote(
            dep.at[g, :, pl.ds(to * slots, slots)], dep_out.at[lat, g, xi],
            d_send.at[g, to], d_recv.at[lat, g, xi], (to // inner, z * inner + to % inner),
        )

    def main_copy(g):
        return remote(gsend.at[g, pl.ds(0, cells)], grecv.at[z], g_send.at[g], g_recv.at[z],
                      (lat, g * inner + xi))

    def halo_copies(g):
        east = (g * inner + xi + 1) % lon_n
        return (
            remote(gsend.at[g, pl.ds(cells, cols)], hrecv.at[0, z], h_send.at[0, g],
                   h_recv.at[0, z], (lat_up, g * inner + xi)),
            remote(gsend.at[g, pl.ds(halo, rows)], hrecv.at[1, z], h_send.at[1, g],
                   h_recv.at[1, z], (lat, east)),
            remote(gsend.at[g, pl.ds(halo + rows, rows)], hrecv.at[2, z], h_send.at[2, g],
                   h_recv.at[2, z], (lat_up, east)),
        )

    def send_meta(i, carry):
        meta_copy(i).start()
        return carry

    def send_tables(i, carry):
        main, north, east, corner = table_copies(i)
        main.start()
        north.start()
        east.start()
        corner.start()
        return carry

    def send_jac(n, carry):
        jac_copy((z + 1 + n // (plane - 1)) % line, 1 + n % (plane - 1)).start()
        return carry

    lax.fori_loop(1, plane, send_meta, 0)
    lax.fori_loop(1, line, send_tables, 0)
    _, north, east, corner = table_copies(0)
    north.start()
    east.start()
    corner.start()
    lax.fori_loop(0, line * (plane - 1), send_jac, 0)

    def wait_meta(k, carry):
        landed(met.at[:, :, pl.ds(k * slots, slots)], m_recv.at[k])
        return carry

    lax.fori_loop(0, plane, wait_meta, 0)
    inside = jnp.where(lat < lat_n - 1, 1.0, 0.0)
    width = tile * slots
    pad = -(-(max(rows, cols) + 1) // 8) * 8

    def group(n, carry):
        g = (z + 1 + n) % line
        landed(tbl.at[g, pl.ds(0, cells)], t_recv.at[0, g])
        landed(tbl.at[g, pl.ds(cells, cols)], t_recv.at[1, g])
        landed(tbl.at[g, pl.ds(halo, rows)], t_recv.at[2, g])
        landed(tbl.at[g, pl.ds(halo + rows, rows)], t_recv.at[3, g])

        def wait_jac(k, inner_carry):
            landed(jrecv.at[g, pl.ds(k * slots, slots)], j_recv.at[g, k])
            return inner_carry

        lax.fori_loop(0, plane, wait_jac, 0)
        grad[...] = jnp.zeros_like(grad)

        def one_tile(t, inner_carry):
            lanes = pl.ds(pl.multiple_of(t * width, width), width)
            info = met[g, :, lanes]
            lat_w = weight_rows(info[0:1], info[2:3], pad)
            lon_w = weight_rows(info[1:2], info[3:4], pad)
            lon_c = lon_w[:cols]
            lon_e = lon_w[cols:cols + 1]
            lat_n_row = lat_w[rows:rows + 1] * inside
            first = lax.broadcasted_iota(jnp.int32, (rows, width), 0) == 0
            blocks = [lat_w[r:r + 1] * lon_c for r in range(rows)]
            blocks.append(lat_n_row * lon_c)
            blocks.append(lat_w[:rows] * lon_e)
            blocks.append(
                jnp.where(first, jnp.broadcast_to(lat_n_row * lon_e, (rows, width)), 0.0)
            )
            spread = jnp.concatenate(blocks, axis=0).astype(jnp.bfloat16).astype(jnp.float32)
            jac_t = jrecv[g, lanes]
            products = lax.dot_general(
                tbl[g], jac_t, (((1,), (1,)), ((), ())), preferred_element_type=jnp.float32
            )
            evolved = jnp.sum(spread * products, axis=0, keepdims=True)
            departure = jnp.where(info[0:1] >= 0.0, evolved - info[4:5], 0.0)
            dep[g, :, lanes] = departure
            scaled = (spread * (info[5:6] * departure)).astype(jnp.bfloat16)
            grad[...] += jnp.dot(scaled, jac_t, preferred_element_type=jnp.float32)
            return inner_carry

        lax.fori_loop(0, plane // tile, one_tile, 0)
        gsend[g] = grad[...].astype(jnp.bfloat16)

        @pl.when(n < line - 1)
        def _():
            main_copy(g).start()

        for copy in halo_copies(g):
            copy.start()

        def send_dep(i, inner_carry):
            dep_copy(g, i).start()
            return inner_carry

        lax.fori_loop(1, plane, send_dep, 0)
        pltpu.make_async_copy(
            dep.at[g, :, pl.ds(here * slots, slots)], dep_out.at[lat, g, xi],
            d_recv.at[lat, g, xi],
        ).start()
        return carry

    lax.fori_loop(0, line, group, 0)

    grad_out[...] = grad[pl.ds(0, cells), :]

    def add_main(i, carry):
        source = (z + i) % line
        landed(grecv.at[source], g_recv.at[source])
        grad_out[...] += grecv[source].astype(jnp.float32)
        return carry

    lax.fori_loop(1, line, add_main, 0)

    def add_halo(s, carry):
        landed(hrecv.at[0, s], h_recv.at[0, s])
        landed(hrecv.at[1, s], h_recv.at[1, s])
        landed(hrecv.at[2, s], h_recv.at[2, s])
        return carry

    lax.fori_loop(0, line, add_halo, 0)
    grad_out[pl.ds(0, cols), :] += jnp.sum(hrecv[0].astype(jnp.float32), axis=0)
    east_sum = jnp.sum(hrecv[1].astype(jnp.float32), axis=0)
    corner_sum = jnp.sum(hrecv[2].astype(jnp.float32), axis=0)
    for r in range(rows):
        extra = east_sum[r:r + 1]
        if r == 0:
            extra = extra + corner_sum[0:1]
        grad_out[pl.ds(r * cols, 1), :] += extra

    def end_dep_recv(n, carry):
        k, g = n // line, n % line
        landed(dep_out.at[k // inner, g, k % inner], d_recv.at[k // inner, g, k % inner])
        return carry

    lax.fori_loop(0, plane * line, end_dep_recv, 0)

    def end_tables(i, carry):
        for copy in table_copies(i):
            copy.wait_send()
        return carry

    lax.fori_loop(1, line, end_tables, 0)
    north.wait_send()
    east.wait_send()
    corner.wait_send()

    def end_meta(i, carry):
        meta_copy(i).wait_send()
        return carry

    lax.fori_loop(1, plane, end_meta, 0)

    def end_blocks(n, carry):
        g, i = n // (plane - 1), 1 + n % (plane - 1)
        jac_copy(g, i).wait_send()
        dep_copy(g, i).wait_send()
        return carry

    lax.fori_loop(0, line * (plane - 1), end_blocks, 0)

    def end_main(i, carry):
        main_copy((z + i) % line).wait_send()
        return carry

    lax.fori_loop(1, line, end_main, 0)

    def end_halo(g, carry):
        for copy in halo_copies(g):
            copy.wait_send()
        return carry

    lax.fori_loop(0, line, end_halo, 0)


def shards(mesh_shape, field, obs_jac, obs_frac, obs_innov, obs_rinv, obs_cells):
    lat_n, lon_n = mesh_shape
    line = math.gcd(lon_n // 2, 4)
    inner = lon_n // line
    plane = lat_n * inner
    rows, cols, wide = field.shape
    slots = obs_jac.shape[2]
    tile = math.gcd(plane, 4)
    cells = rows * cols
    table = cells + cols + 2 * rows

    ids = obs_cells[:, 0]
    live = ids >= 0
    f32 = jnp.float32
    away = jnp.asarray(-1000.0, f32)
    row_pos = jnp.where(live, (ids // (cols + 1)).astype(f32), away)
    col_pos = jnp.where(live, (ids % (cols + 1)).astype(f32), away)
    none = jnp.zeros_like(row_pos)
    meta = jnp.stack(
        [row_pos, col_pos, obs_frac[:, 0, 0].astype(f32), obs_frac[:, 0, 1].astype(f32),
         obs_innov[:, 0].astype(f32), obs_rinv[:, 0].astype(f32), none, none],
        axis=1,
    ).reshape(lat_n, line, inner, 8, slots)
    jac = obs_jac.reshape(lat_n, line, inner, slots, wide)
    bf16 = jnp.bfloat16
    dma = pltpu.SemaphoreType.DMA
    vmem = pl.BlockSpec(memory_space=pltpu.VMEM)
    grad, departures = pl.pallas_call(
        functools.partial(kernel, lat_n, lon_n, line, rows, cols, tile),
        out_shape=(
            jax.ShapeDtypeStruct((cells, wide), f32),
            jax.ShapeDtypeStruct((lat_n, line, inner, 1, slots), f32),
        ),
        in_specs=[vmem, vmem, vmem, pl.BlockSpec(memory_space=pl.ANY)],
        out_specs=(vmem, vmem),
        scratch_shapes=[
            pltpu.VMEM((line, table, wide), bf16),
            pltpu.VMEM((line, 8, plane * slots), f32),
            pltpu.VMEM((line, plane * slots, wide), bf16),
            pltpu.VMEM((line, 1, plane * slots), f32),
            pltpu.VMEM((table, wide), f32),
            pltpu.VMEM((line, table, wide), bf16),
            pltpu.VMEM((line, cells, wide), bf16),
            pltpu.VMEM((3, line, rows, wide), bf16),
            dma((4, line)), dma((4, line)),
            dma((plane,)), dma((plane,)),
            dma((line, plane)), dma((line, plane)),
            dma((line, plane)), dma((lat_n, line, inner)),
            dma((line,)), dma((line,)),
            dma((3, line)), dma((3, line)),
        ],
        compiler_params=pltpu.CompilerParams(
            collective_id=0, has_side_effects=True, vmem_limit_bytes=60 * 1024 * 1024
        ),
    )(field.reshape(cells, wide), field[:, 0], meta, jac)
    return (
        departures.reshape(lat_n * lon_n, 1, slots),
        grad.reshape(rows, cols, wide),
    )


def solution(mesh):
    placed = (
        P("lat", "lon", None),
        P(None, ("lat", "lon"), None, None),
        P(None, ("lat", "lon"), None, None),
        P(None, ("lat", "lon"), None),
        P(None, ("lat", "lon"), None),
        P(None, ("lat", "lon"), None),
    )
    return jax.shard_map(
        functools.partial(shards, (mesh.shape["lat"], mesh.shape["lon"])),
        mesh=mesh,
        in_specs=placed,
        out_specs=(P(None, ("lat", "lon"), None), P("lat", "lon", None)),
        check_vma=False,
    )
```

```python
import functools
import math

import jax
import jax.numpy as jnp
from jax import lax
from jax.experimental import pallas as pl
from jax.experimental.pallas import tpu as pltpu
from jax.sharding import PartitionSpec as P

MESH = pl.DeviceIdType.MESH
AWAY = -1000.0


def weight_rows(position, frac, rows):
    ids = lax.broadcasted_iota(jnp.int32, (rows, position.shape[1]), 0).astype(jnp.float32)
    zero = jnp.zeros_like(ids)
    return jnp.where(
        ids == position, 1.0 - frac, jnp.where(ids == position + 1.0, frac, zero)
    )


def kernel(
    lat_n, lon_n, line, rows, cols, tile,
    field, cell_ref, frac_ref, innov_ref, rinv_ref, jac,
    grad_out, dep_out,
    edge, innov, rinv, meta,
    tbl, met, jrecv, dep, grad, gsend, grecv, hrecv,
    t_send, t_recv, m_send, m_recv, j_send, j_recv, d_send, d_recv,
    g_send, g_recv, h_send, h_recv,
):
    inner = lon_n // line
    plane = lat_n * inner
    total = lat_n * lon_n
    slots = jac.shape[3]
    cells = rows * cols
    halo = cells + cols
    lat, lon = lax.axis_index("lat"), lax.axis_index("lon")
    z, xi = lon // inner, lon % inner
    here = lat * inner + xi
    lat_up, lat_down = (lat + 1) % lat_n, (lat + lat_n - 1) % lat_n
    lon_down = (lon + lon_n - 1) % lon_n
    z_low, x_low = lon_down // inner, lon_down % inner

    def remote(src, dst, send, recv, to):
        return pltpu.make_async_remote_copy(
            src_ref=src, dst_ref=dst, send_sem=send, recv_sem=recv,
            device_id=to, device_id_type=MESH,
        )

    def landed(like, sem):
        pltpu.make_async_copy(like, like, sem).wait()

    me = lat * lon_n + lon
    barrier = pltpu.get_barrier_semaphore()

    def greet(i, carry):
        other = (me + i) % total
        pl.semaphore_signal(
            barrier, inc=1, device_id=(other // lon_n, other % lon_n), device_id_type=MESH
        )
        return carry

    lax.fori_loop(1, total, greet, 0)

    mine = pl.ds(here * slots, slots)
    pltpu.make_async_copy(field, tbl.at[z, pl.ds(0, cells)], t_recv.at[z]).start()
    for n in range(line):
        g = (z + 1 + n) % line
        pltpu.make_async_copy(jac.at[lat, g, xi], jrecv.at[g, mine], j_recv.at[g]).start()
    edge[...] = jnp.concatenate(
        [field[pl.ds(r * cols, cols), :].astype(jnp.float32)[0:1] for r in range(rows)], axis=0
    ).astype(edge.dtype)
    innov[...] = innov_ref[...].astype(jnp.float32)
    rinv[...] = rinv_ref[...].astype(jnp.float32)

    def build(k, carry):
        for g in range(line):
            owner = (k // inner) * lon_n + g * inner + k % inner
            cell = cell_ref[owner].astype(jnp.float32)
            live = cell >= 0.0
            row = jnp.floor((cell + 0.5) * (1.0 / (cols + 1)))
            meta[k, g, 0:1] = jnp.where(live, row, AWAY)
            meta[k, g, 1:2] = jnp.where(live, cell - row * (cols + 1), AWAY)
            meta[k, g, 2:4] = frac_ref[owner].astype(jnp.float32)
            meta[k, g, 4:5] = innov[pl.ds(owner, 1), :]
            meta[k, g, 5:6] = rinv[pl.ds(owner, 1), :]
            meta[k, g, 6:8] = jnp.zeros((2, slots), jnp.float32)
        return carry

    lax.fori_loop(0, plane, build, 0)
    pltpu.make_async_copy(meta.at[here], met.at[:, :, mine], m_recv).start()
    pl.semaphore_wait(barrier, total - 1)

    def send_jac(g):
        def one(i, carry):
            to = (here + i) % plane
            remote(
                jac.at[to // inner, g, to % inner], jrecv.at[g, mine], j_send, j_recv.at[g],
                (to // inner, z * inner + to % inner),
            ).start()
            return carry

        lax.fori_loop(1, plane, one, 0)

    def send_meta(i, carry):
        to = (here + i) % plane
        remote(
            meta.at[to], met.at[:, :, mine], m_send, m_recv,
            (to // inner, z * inner + to % inner),
        ).start()
        return carry

    send_jac((z + 1) % line)
    for i in (*range(1, line), 0):
        to = (z + i) % line
        if i > 0:
            remote(field, tbl.at[z, pl.ds(0, cells)], t_send.at[0], t_recv.at[z],
                   (lat, to * inner + xi)).start()
        remote(field.at[pl.ds(0, cols)], tbl.at[z, pl.ds(cells, cols)], t_send.at[1],
               t_recv.at[z], (lat_down, to * inner + xi)).start()
        remote(edge, tbl.at[z_low, pl.ds(halo, rows)], t_send.at[1], t_recv.at[z_low],
               (lat, to * inner + x_low)).start()
        remote(edge, tbl.at[z_low, pl.ds(halo + rows, rows)], t_send.at[1], t_recv.at[z_low],
               (lat_down, to * inner + x_low)).start()
    lax.fori_loop(1, plane, send_meta, 0)
    for n in range(1, line):
        send_jac((z + 1 + n) % line)

    landed(met, m_recv)
    inside = jnp.where(lat < lat_n - 1, 1.0, 0.0)
    width = tile * slots
    tiles = plane // tile
    pad = -(-(max(rows, cols) + 1) // 8) * 8

    def group(n, carry):
        g = (z + 1 + n) % line
        landed(tbl.at[g], t_recv.at[g])
        landed(jrecv.at[g], j_recv.at[g])
        if tiles > 1:
            grad[...] = jnp.zeros_like(grad)

        def one_tile(t, inner_carry):
            lanes = pl.ds(pl.multiple_of(t * width, width), width)
            info = met[g, :, lanes]
            lat_w = weight_rows(info[0:1], info[2:3], pad)
            lon_w = weight_rows(info[1:2], info[3:4], pad)
            lon_c = lon_w[:cols]
            lon_e = lon_w[cols:cols + 1]
            lat_n_row = lat_w[rows:rows + 1] * inside
            first = lax.broadcasted_iota(jnp.int32, (rows, width), 0) == 0
            blocks = [lat_w[r:r + 1] * lon_c for r in range(rows)]
            blocks.append(lat_n_row * lon_c)
            blocks.append(lat_w[:rows] * lon_e)
            blocks.append(
                jnp.where(first, jnp.broadcast_to(lat_n_row * lon_e, (rows, width)), 0.0)
            )
            spread = jnp.concatenate(blocks, axis=0).astype(jnp.bfloat16).astype(jnp.float32)
            jac_t = jrecv[g, lanes]
            products = lax.dot_general(
                tbl[g], jac_t, (((1,), (1,)), ((), ())), preferred_element_type=jnp.float32
            )
            evolved = jnp.sum(spread * products, axis=0, keepdims=True)
            departure = jnp.where(info[0:1] >= 0.0, evolved - info[4:5], 0.0)
            dep[g, :, lanes] = departure
            scaled = (spread * (info[5:6] * departure)).astype(jnp.bfloat16)
            partial = jnp.dot(scaled, jac_t, preferred_element_type=jnp.float32)
            if tiles > 1:
                grad[...] += partial
            else:
                grad[...] = partial
            return inner_carry

        if tiles > 1:
            lax.fori_loop(0, tiles, one_tile, 0)
        else:
            one_tile(0, 0)
        gsend[g] = grad[...].astype(jnp.bfloat16)
        east = (g * inner + xi + 1) % lon_n
        remote(gsend.at[g, pl.ds(cells, cols)], hrecv.at[0, z], h_send, h_recv,
               (lat_up, g * inner + xi)).start()
        remote(gsend.at[g, pl.ds(halo, rows)], hrecv.at[1, z], h_send, h_recv,
               (lat, east)).start()
        remote(gsend.at[g, pl.ds(halo + rows, rows)], hrecv.at[2, z], h_send, h_recv,
               (lat_up, east)).start()

        @pl.when(n < line - 1)
        def _():
            slot = lax.rem(n, line - 1)
            remote(gsend.at[g, pl.ds(0, cells)], grecv.at[slot], g_send, g_recv,
                   (lat, g * inner + xi)).start()

        def send_dep(i, inner_carry):
            to = (here + i) % plane
            remote(
                dep.at[g, :, pl.ds(to * slots, slots)], dep_out.at[lat, g, xi], d_send, d_recv,
                (to // inner, z * inner + to % inner),
            ).start()
            return inner_carry

        lax.fori_loop(1, plane, send_dep, 0)
        pltpu.make_async_copy(dep.at[g, :, mine], dep_out.at[lat, g, xi], d_recv).start()
        return carry

    lax.fori_loop(0, line, group, 0)

    landed(grecv, g_recv)
    field_sum = grad[pl.ds(0, cells), :]
    for slot in range(line - 1):
        field_sum = field_sum + grecv[slot].astype(jnp.float32)
    grad_out[...] = field_sum
    landed(hrecv, h_recv)
    grad_out[pl.ds(0, cols), :] += jnp.sum(hrecv[0].astype(jnp.float32), axis=0)
    east_sum = jnp.sum(hrecv[1].astype(jnp.float32), axis=0)
    corner_sum = jnp.sum(hrecv[2].astype(jnp.float32), axis=0)
    for r in range(rows):
        extra = east_sum[r:r + 1]
        if r == 0:
            extra = extra + corner_sum[0:1]
        grad_out[pl.ds(r * cols, 1), :] += extra

    others = pl.ds(0, (plane - 1) * slots)
    landed(dep_out, d_recv)
    landed(grecv, t_send.at[0])
    landed(tbl.at[:, pl.ds(cells, cols + 2 * rows)], t_send.at[1])
    landed(met.at[:, :, others], m_send)
    landed(jrecv.at[:, others], j_send)
    landed(dep.at[:, :, others], d_send)
    landed(grecv, g_send)
    landed(gsend.at[:, pl.ds(cells, cols + 2 * rows)], h_send)


def shards(mesh_shape, field, obs_jac, obs_frac, obs_innov, obs_rinv, obs_cells):
    lat_n, lon_n = mesh_shape
    line = math.gcd(lon_n // 2, 4)
    inner = lon_n // line
    plane = lat_n * inner
    total = lat_n * lon_n
    rows, cols, wide = field.shape
    slots = obs_jac.shape[2]
    tile = math.gcd(plane, 8)
    cells = rows * cols
    table = cells + cols + 2 * rows
    f32, bf16 = jnp.float32, jnp.bfloat16
    dma = pltpu.SemaphoreType.DMA
    one = pltpu.SemaphoreType.DMA(())
    vmem = pl.BlockSpec(memory_space=pltpu.VMEM)
    grad, departures = pl.pallas_call(
        functools.partial(kernel, lat_n, lon_n, line, rows, cols, tile),
        out_shape=(
            jax.ShapeDtypeStruct((cells, wide), f32),
            jax.ShapeDtypeStruct((lat_n, line, inner, 1, slots), f32),
        ),
        in_specs=[vmem, vmem, vmem, vmem, vmem, pl.BlockSpec(memory_space=pl.ANY)],
        out_specs=(vmem, vmem),
        scratch_shapes=[
            pltpu.VMEM((rows, wide), bf16),
            pltpu.VMEM((total, slots), f32),
            pltpu.VMEM((total, slots), f32),
            pltpu.VMEM((plane, line, 8, slots), f32),
            pltpu.VMEM((line, table, wide), bf16),
            pltpu.VMEM((line, 8, plane * slots), f32),
            pltpu.VMEM((line, plane * slots, wide), bf16),
            pltpu.VMEM((line, 1, plane * slots), f32),
            pltpu.VMEM((table, wide), f32),
            pltpu.VMEM((line, table, wide), bf16),
            pltpu.VMEM((line - 1, cells, wide), bf16),
            pltpu.VMEM((3, line, rows, wide), bf16),
            dma((2,)), dma((line,)),
            one, one,
            one, dma((line,)),
            one, one,
            one, one,
            one, one,
        ],
        compiler_params=pltpu.CompilerParams(
            collective_id=0, has_side_effects=True, vmem_limit_bytes=60 * 1024 * 1024
        ),
    )(
        field.reshape(cells, wide),
        obs_cells,
        obs_frac.reshape(total, 2, slots),
        obs_innov.reshape(total, slots),
        obs_rinv.reshape(total, slots),
        obs_jac.reshape(lat_n, line, inner, slots, wide),
    )
    return (
        departures.reshape(total, 1, slots),
        grad.reshape(rows, cols, wide),
    )


def solution(mesh):
    placed = (
        P("lat", "lon", None),
        P(None, ("lat", "lon"), None, None),
        P(None, ("lat", "lon"), None, None),
        P(None, ("lat", "lon"), None),
        P(None, ("lat", "lon"), None),
        P(None, ("lat", "lon"), None),
    )
    return jax.shard_map(
        functools.partial(shards, (mesh.shape["lat"], mesh.shape["lon"])),
        mesh=mesh,
        in_specs=placed,
        out_specs=(P(None, ("lat", "lon"), None), P("lat", "lon", None)),
        check_vma=False,
    )
```

```python
import functools
import math

import jax
import jax.numpy as jnp
from jax import lax
from jax.experimental import pallas as pl
from jax.experimental.pallas import tpu as pltpu
from jax.sharding import PartitionSpec as P

MESH = pl.DeviceIdType.MESH
AWAY = -1000.0


def weight_rows(position, frac, rows):
    ids = lax.broadcasted_iota(jnp.int32, (rows, position.shape[1]), 0).astype(jnp.float32)
    zero = jnp.zeros_like(ids)
    return jnp.where(
        ids == position, 1.0 - frac, jnp.where(ids == position + 1.0, frac, zero)
    )


def kernel(
    lat_n, lon_n, line, rows, cols, tile,
    field, cell_ref, frac_ref, innov_ref, rinv_ref, jac,
    grad, grecv, hrecv, dep_out,
    edge, innov, rinv, meta,
    tbl, met, jrecv, dep, gsend,
    t_send, t_recv, m_send, m_recv, j_send, j_recv, d_send, d_recv,
    g_send, g_recv, h_send, h_recv, from_low, from_high,
):
    inner = lon_n // line
    plane = lat_n * inner
    total = lat_n * lon_n
    slots = jac.shape[3]
    cells = rows * cols
    halo = cells + cols
    lat, lon = lax.axis_index("lat"), lax.axis_index("lon")
    z, xi = lon // inner, lon % inner
    here = lat * inner + xi
    lat_up, lat_down = (lat + 1) % lat_n, (lat + lat_n - 1) % lat_n
    lon_down = (lon + lon_n - 1) % lon_n
    z_low, x_low = lon_down // inner, lon_down % inner

    def remote(src, dst, send, recv, to):
        return pltpu.make_async_remote_copy(
            src_ref=src, dst_ref=dst, send_sem=send, recv_sem=recv,
            device_id=to, device_id_type=MESH,
        )

    def landed(like, sem):
        pltpu.make_async_copy(like, like, sem).wait()

    has_low, has_high = z > 0, z < line - 1
    low, high = (lat, lon - inner), (lat, lon + inner)
    barrier = pltpu.get_barrier_semaphore()

    @pl.when(has_low)
    def _():
        pl.semaphore_signal(barrier, inc=1, device_id=low, device_id_type=MESH)

    @pl.when(has_high)
    def _():
        pl.semaphore_signal(barrier, inc=1, device_id=high, device_id_type=MESH)

    def greet(i, carry):
        to = (here + i) % plane
        pl.semaphore_signal(
            barrier, inc=1, device_id=(to // inner, z * inner + to % inner), device_id_type=MESH
        )
        return carry

    lax.fori_loop(1, plane, greet, 0)

    mine = pl.ds(here * slots, slots)
    pltpu.make_async_copy(field, tbl.at[z, pl.ds(0, cells)], t_recv.at[z]).start()
    for n in range(line):
        g = (z + 1 + n) % line
        pltpu.make_async_copy(jac.at[lat, g, xi], jrecv.at[g, mine], j_recv.at[g]).start()
    pl.semaphore_wait(barrier, plane - 1 + has_low.astype(jnp.int32) + has_high.astype(jnp.int32))

    def send_jac(g):
        def one(i, carry):
            to = (here + i) % plane
            remote(
                jac.at[to // inner, g, to % inner], jrecv.at[g, mine], j_send, j_recv.at[g],
                (to // inner, z * inner + to % inner),
            ).start()
            return carry

        lax.fori_loop(1, plane, one, 0)

    def send_meta(i, carry):
        to = (here + i) % plane
        remote(
            meta.at[to], met.at[:, :, mine], m_send, m_recv,
            (to // inner, z * inner + to % inner),
        ).start()
        return carry

    send_jac((z + 1) % line)
    edge[...] = jnp.concatenate(
        [field[pl.ds(r * cols, cols), :].astype(jnp.float32)[0:1] for r in range(rows)], axis=0
    ).astype(edge.dtype)

    for _ in range(line - 1):
        @pl.when(has_low)
        def _():
            pl.semaphore_signal(from_high, inc=1, device_id=low, device_id_type=MESH)

        @pl.when(has_high)
        def _():
            pl.semaphore_signal(from_low, inc=1, device_id=high, device_id_type=MESH)

        @pl.when(has_low)
        def _():
            pl.semaphore_wait(from_low, 1)

        @pl.when(has_high)
        def _():
            pl.semaphore_wait(from_high, 1)

    for i in (*range(1, line), 0):
        to = (z + i) % line
        if i > 0:
            remote(field, tbl.at[z, pl.ds(0, cells)], t_send.at[0], t_recv.at[z],
                   (lat, to * inner + xi)).start()
        remote(field.at[pl.ds(0, cols)], tbl.at[z, pl.ds(cells, cols)], t_send.at[1],
               t_recv.at[z], (lat_down, to * inner + xi)).start()
        remote(edge, tbl.at[z_low, pl.ds(halo, rows)], t_send.at[1], t_recv.at[z_low],
               (lat, to * inner + x_low)).start()
        remote(edge, tbl.at[z_low, pl.ds(halo + rows, rows)], t_send.at[1], t_recv.at[z_low],
               (lat_down, to * inner + x_low)).start()
    send_jac((z + 2) % line)
    innov[...] = innov_ref[...].astype(jnp.float32)
    rinv[...] = rinv_ref[...].astype(jnp.float32)

    def build(k, carry):
        for g in range(line):
            owner = (k // inner) * lon_n + g * inner + k % inner
            cell = cell_ref[owner].astype(jnp.float32)
            live = cell >= 0.0
            row = jnp.floor((cell + 0.5) * (1.0 / (cols + 1)))
            meta[k, g, 0:1] = jnp.where(live, row, AWAY)
            meta[k, g, 1:2] = jnp.where(live, cell - row * (cols + 1), AWAY)
            meta[k, g, 2:4] = frac_ref[owner].astype(jnp.float32)
            meta[k, g, 4:5] = innov[pl.ds(owner, 1), :]
            meta[k, g, 5:6] = rinv[pl.ds(owner, 1), :]
            meta[k, g, 6:8] = jnp.zeros((2, slots), jnp.float32)
        return carry

    lax.fori_loop(0, plane, build, 0)
    pltpu.make_async_copy(meta.at[here], met.at[:, :, mine], m_recv).start()

    lax.fori_loop(1, plane, send_meta, 0)
    for n in range(2, line):
        send_jac((z + 1 + n) % line)

    landed(met, m_recv)
    inside = jnp.where(lat < lat_n - 1, 1.0, 0.0)
    width = tile * slots
    tiles = plane // tile
    pad = -(-(max(rows, cols) + 1) // 8) * 8

    def group(n, carry):
        g = (z + 1 + n) % line
        landed(tbl.at[g], t_recv.at[g])
        landed(jrecv.at[g], j_recv.at[g])
        if tiles > 1:
            grad[...] = jnp.zeros_like(grad)

        def one_tile(t, inner_carry):
            lanes = pl.ds(pl.multiple_of(t * width, width), width)
            info = met[g, :, lanes]
            lat_w = weight_rows(info[0:1], info[2:3], pad)
            lon_w = weight_rows(info[1:2], info[3:4], pad)
            lon_c = lon_w[:cols]
            lon_e = lon_w[cols:cols + 1]
            lat_n_row = lat_w[rows:rows + 1] * inside
            first = lax.broadcasted_iota(jnp.int32, (rows, width), 0) == 0
            blocks = [lat_w[r:r + 1] * lon_c for r in range(rows)]
            blocks.append(lat_n_row * lon_c)
            blocks.append(lat_w[:rows] * lon_e)
            blocks.append(
                jnp.where(first, jnp.broadcast_to(lat_n_row * lon_e, (rows, width)), 0.0)
            )
            spread = jnp.concatenate(blocks, axis=0).astype(jnp.bfloat16).astype(jnp.float32)
            jac_t = jrecv[g, lanes]
            products = lax.dot_general(
                tbl[g], jac_t, (((1,), (1,)), ((), ())), preferred_element_type=jnp.float32
            )
            evolved = jnp.sum(spread * products, axis=0, keepdims=True)
            departure = jnp.where(info[0:1] >= 0.0, evolved - info[4:5], 0.0)
            dep[g, :, lanes] = departure
            scaled = (spread * (info[5:6] * departure)).astype(jnp.bfloat16)
            partial = jnp.dot(scaled, jac_t, preferred_element_type=jnp.float32)
            if tiles > 1:
                grad[...] += partial
            else:
                grad[...] = partial
            return inner_carry

        if tiles > 1:
            lax.fori_loop(0, tiles, one_tile, 0)
        else:
            one_tile(0, 0)
        gsend[g] = grad[...].astype(jnp.bfloat16)
        east = (g * inner + xi + 1) % lon_n
        remote(gsend.at[g, pl.ds(cells, cols)], hrecv.at[0, z], h_send, h_recv,
               (lat_up, g * inner + xi)).start()
        remote(gsend.at[g, pl.ds(halo, rows)], hrecv.at[1, z], h_send, h_recv,
               (lat, east)).start()
        remote(gsend.at[g, pl.ds(halo + rows, rows)], hrecv.at[2, z], h_send, h_recv,
               (lat_up, east)).start()

        @pl.when(n < line - 1)
        def _():
            slot = lax.rem(n, line - 1)
            remote(gsend.at[g, pl.ds(0, cells)], grecv.at[slot], g_send, g_recv,
                   (lat, g * inner + xi)).start()

        def send_dep(i, inner_carry):
            to = (here + i) % plane
            remote(
                dep.at[g, :, pl.ds(to * slots, slots)], dep_out.at[lat, g, xi], d_send, d_recv,
                (to // inner, z * inner + to % inner),
            ).start()
            return inner_carry

        lax.fori_loop(1, plane, send_dep, 0)
        pltpu.make_async_copy(dep.at[g, :, mine], dep_out.at[lat, g, xi], d_recv).start()
        return carry

    lax.fori_loop(0, line, group, 0)

    others = pl.ds(0, (plane - 1) * slots)
    landed(grecv, g_recv)
    landed(hrecv, h_recv)
    landed(dep_out, d_recv)
    landed(grecv, t_send.at[0])
    landed(tbl.at[:, pl.ds(cells, cols + 2 * rows)], t_send.at[1])
    landed(met.at[:, :, others], m_send)
    landed(jrecv.at[:, others], j_send)
    landed(dep.at[:, :, others], d_send)
    landed(grecv, g_send)
    landed(gsend.at[:, pl.ds(cells, cols + 2 * rows)], h_send)


def last_sums(rows, cols, grad, grecv, hrecv, dep, grad_out, dep_out):
    dep_out[...] = dep[...]
    field_sum = grad[pl.ds(0, rows * cols), :]
    for slot in range(grecv.shape[0]):
        field_sum = field_sum + grecv[slot].astype(jnp.float32)
    grad_out[...] = field_sum
    grad_out[pl.ds(0, cols), :] += jnp.sum(hrecv[0].astype(jnp.float32), axis=0)
    east_sum = jnp.sum(hrecv[1].astype(jnp.float32), axis=0)
    corner_sum = jnp.sum(hrecv[2].astype(jnp.float32), axis=0)
    for r in range(rows):
        extra = east_sum[r:r + 1]
        if r == 0:
            extra = extra + corner_sum[0:1]
        grad_out[pl.ds(r * cols, 1), :] += extra


def shards(mesh_shape, field, obs_jac, obs_frac, obs_innov, obs_rinv, obs_cells):
    lat_n, lon_n = mesh_shape
    line = math.gcd(lon_n // 2, 4)
    inner = lon_n // line
    plane = lat_n * inner
    total = lat_n * lon_n
    rows, cols, wide = field.shape
    slots = obs_jac.shape[2]
    tile = math.gcd(plane, 8)
    cells = rows * cols
    table = cells + cols + 2 * rows
    f32, bf16 = jnp.float32, jnp.bfloat16
    dma = pltpu.SemaphoreType.DMA
    one = pltpu.SemaphoreType.DMA(())
    vmem = pl.BlockSpec(memory_space=pltpu.VMEM)
    parts = pl.pallas_call(
        functools.partial(kernel, lat_n, lon_n, line, rows, cols, tile),
        out_shape=(
            jax.ShapeDtypeStruct((table, wide), f32),
            jax.ShapeDtypeStruct((line - 1, cells, wide), bf16),
            jax.ShapeDtypeStruct((3, line, rows, wide), bf16),
            jax.ShapeDtypeStruct((lat_n, line, inner, 1, slots), f32),
        ),
        in_specs=[vmem, vmem, vmem, vmem, vmem, pl.BlockSpec(memory_space=pl.ANY)],
        out_specs=(vmem,) * 4,
        scratch_shapes=[
            pltpu.VMEM((rows, wide), bf16),
            pltpu.VMEM((total, slots), f32),
            pltpu.VMEM((total, slots), f32),
            pltpu.VMEM((plane, line, 8, slots), f32),
            pltpu.VMEM((line, table, wide), bf16),
            pltpu.VMEM((line, 8, plane * slots), f32),
            pltpu.VMEM((line, plane * slots, wide), bf16),
            pltpu.VMEM((line, 1, plane * slots), f32),
            pltpu.VMEM((line, table, wide), bf16),
            dma((2,)), dma((line,)),
            one, one,
            one, dma((line,)),
            one, one,
            one, one,
            one, one,
            pltpu.SemaphoreType.REGULAR, pltpu.SemaphoreType.REGULAR,
        ],
        compiler_params=pltpu.CompilerParams(
            collective_id=0, has_side_effects=True, vmem_limit_bytes=60 * 1024 * 1024
        ),
    )(
        field.reshape(cells, wide),
        obs_cells,
        obs_frac.reshape(total, 2, slots),
        obs_innov.reshape(total, slots),
        obs_rinv.reshape(total, slots),
        obs_jac.reshape(lat_n, line, inner, slots, wide),
    )
    grad, departures = pl.pallas_call(
        functools.partial(last_sums, rows, cols),
        out_shape=(
            jax.ShapeDtypeStruct((cells, wide), f32),
            jax.ShapeDtypeStruct((total, 1, slots), f32),
        ),
        in_specs=[vmem] * 4,
        out_specs=(vmem, vmem),
    )(*parts[:3], parts[3].reshape(total, 1, slots))
    return departures, grad.reshape(rows, cols, wide)


def solution(mesh):
    placed = (
        P("lat", "lon", None),
        P(None, ("lat", "lon"), None, None),
        P(None, ("lat", "lon"), None, None),
        P(None, ("lat", "lon"), None),
        P(None, ("lat", "lon"), None),
        P(None, ("lat", "lon"), None),
    )
    return jax.shard_map(
        functools.partial(shards, (mesh.shape["lat"], mesh.shape["lon"])),
        mesh=mesh,
        in_specs=placed,
        out_specs=(P(None, ("lat", "lon"), None), P("lat", "lon", None)),
        check_vma=False,
    )
```

```python
import functools
import math

import jax
import jax.numpy as jnp
from jax import lax
from jax.experimental import pallas as pl
from jax.experimental.pallas import tpu as pltpu
from jax.sharding import PartitionSpec as P

MESH = pl.DeviceIdType.MESH
AWAY = -1000.0


def weight_rows(position, frac, rows):
    ids = lax.broadcasted_iota(jnp.int32, (rows, position.shape[1]), 0).astype(jnp.float32)
    zero = jnp.zeros_like(ids)
    return jnp.where(
        ids == position, 1.0 - frac, jnp.where(ids == position + 1.0, frac, zero)
    )


def kernel(
    lat_n, lon_n, line, rows, cols, tile,
    field, cell_ref, frac_ref, innov_ref, rinv_ref, jac,
    grad, grecv, hrecv, dep_out,
    edge, innov, rinv, meta,
    tbl, met, jrecv, dep, gsend,
    e_send, t_send, t_recv, m_send, m_recv, j_send, j_recv, d_send, d_recv,
    g_send, g_recv, h_send, h_recv, from_low, from_high,
):
    inner = lon_n // line
    plane = lat_n * inner
    total = lat_n * lon_n
    slots = jac.shape[3]
    cells = rows * cols
    halo = cells + cols
    lat, lon = lax.axis_index("lat"), lax.axis_index("lon")
    z, xi = lon // inner, lon % inner
    here = lat * inner + xi
    lat_up, lat_down = (lat + 1) % lat_n, (lat + lat_n - 1) % lat_n
    lon_down = (lon + lon_n - 1) % lon_n
    z_low, x_low = lon_down // inner, lon_down % inner

    step = 2 * (2 * z < line).astype(jnp.int32) - 1

    def band(n):
        return (z + step * (n + 1) + line) % line

    def remote(src, dst, send, recv, to):
        return pltpu.make_async_remote_copy(
            src_ref=src, dst_ref=dst, send_sem=send, recv_sem=recv,
            device_id=to, device_id_type=MESH,
        )

    def landed(like, sem):
        pltpu.make_async_copy(like, like, sem).wait()

    has_low, has_high = z > 0, z < line - 1
    low, high = (lat, lon - inner), (lat, lon + inner)
    barrier = pltpu.get_barrier_semaphore()

    @pl.when(has_low)
    def _():
        pl.semaphore_signal(barrier, inc=1, device_id=low, device_id_type=MESH)

    @pl.when(has_high)
    def _():
        pl.semaphore_signal(barrier, inc=1, device_id=high, device_id_type=MESH)

    def greet(i, carry):
        to = (here + i) % plane
        pl.semaphore_signal(
            barrier, inc=1, device_id=(to // inner, z * inner + to % inner), device_id_type=MESH
        )
        return carry

    lax.fori_loop(1, plane, greet, 0)

    mine = pl.ds(here * slots, slots)
    pltpu.make_async_copy(field, tbl.at[z, pl.ds(0, cells)], t_recv.at[z]).start()
    for n in range(line):
        g = band(n)
        pltpu.make_async_copy(jac.at[lat, g, xi], jrecv.at[g, mine], j_recv.at[g]).start()
    pl.semaphore_wait(barrier, plane - 1 + has_low.astype(jnp.int32) + has_high.astype(jnp.int32))

    def send_jac(g):
        def one(i, carry):
            to = (here + i) % plane
            remote(
                jac.at[to // inner, g, to % inner], jrecv.at[g, mine], j_send, j_recv.at[g],
                (to // inner, z * inner + to % inner),
            ).start()
            return carry

        lax.fori_loop(1, plane, one, 0)

    def send_meta(i, carry):
        to = (here + i) % plane
        remote(
            meta.at[to], met.at[:, :, mine], m_send, m_recv,
            (to // inner, z * inner + to % inner),
        ).start()
        return carry

    send_jac(band(0))
    edge[...] = jnp.concatenate(
        [field[pl.ds(r * cols, cols), :].astype(jnp.float32)[0:1] for r in range(rows)], axis=0
    ).astype(edge.dtype)

    for turn in range(line - 1):
        @pl.when(has_low)
        def _():
            pl.semaphore_signal(from_high, inc=1, device_id=low, device_id_type=MESH)

        @pl.when(has_high)
        def _():
            pl.semaphore_signal(from_low, inc=1, device_id=high, device_id_type=MESH)

        @pl.when(has_low)
        def _():
            pl.semaphore_wait(from_low, 1)

        @pl.when(has_high)
        def _():
            pl.semaphore_wait(from_high, 1)

        if turn == 0:
            remote(field.at[pl.ds(0, cols)], tbl.at[z, pl.ds(cells, cols)], e_send,
                   t_recv.at[z], (lat_down, lon)).start()
        if turn == line - 2:
            remote(edge, tbl.at[z_low, pl.ds(halo, rows)], e_send, t_recv.at[z_low],
                   (lat, lon_down)).start()
            remote(edge, tbl.at[z_low, pl.ds(halo + rows, rows)], e_send, t_recv.at[z_low],
                   (lat_down, lon_down)).start()

    def to_high(slot):
        return remote(tbl.at[slot], tbl.at[slot], t_send.at[0, slot], t_recv.at[slot], high)

    def to_low(slot):
        return remote(tbl.at[slot], tbl.at[slot], t_send.at[1, slot], t_recv.at[slot], low)

    def pass_on(n):
        below, above = z - n - 1, z + n + 1

        @pl.when(below >= 0)
        def _():
            landed(tbl.at[below], t_recv.at[below])

            @pl.when(has_high)
            def _():
                to_high(below).start()

        @pl.when(above < line)
        def _():
            landed(tbl.at[above], t_recv.at[above])

            @pl.when(has_low)
            def _():
                to_low(above).start()

    send_jac(band(1))
    innov[...] = innov_ref[...].astype(jnp.float32)
    rinv[...] = rinv_ref[...].astype(jnp.float32)

    def build(k, carry):
        for g in range(line):
            owner = (k // inner) * lon_n + g * inner + k % inner
            cell = cell_ref[owner].astype(jnp.float32)
            live = cell >= 0.0
            row = jnp.floor((cell + 0.5) * (1.0 / (cols + 1)))
            meta[k, g] = jnp.concatenate(
                [
                    jnp.where(live, row, AWAY),
                    jnp.where(live, cell - row * (cols + 1), AWAY),
                    frac_ref[owner].astype(jnp.float32),
                    innov[pl.ds(owner, 1), :],
                    rinv[pl.ds(owner, 1), :],
                    jnp.zeros((2, slots), jnp.float32),
                ],
                axis=0,
            ).astype(meta.dtype)
        return carry

    lax.fori_loop(0, plane, build, 0)
    pltpu.make_async_copy(meta.at[here], met.at[:, :, mine], m_recv).start()

    landed(tbl.at[z], t_recv.at[z])

    @pl.when(has_high)
    def _():
        to_high(z).start()

    @pl.when(has_low)
    def _():
        to_low(z).start()

    lax.fori_loop(1, plane, send_meta, 0)
    for n in range(2, line):
        send_jac(band(n))

    landed(met, m_recv)
    inside = jnp.where(lat < lat_n - 1, 1.0, 0.0)
    width = tile * slots
    tiles = plane // tile
    pad = -(-(max(rows, cols) + 1) // 8) * 8

    def group(n, carry):
        g = band(n)

        @pl.when(n < line - 1)
        def _():
            pass_on(n)

        landed(jrecv.at[g], j_recv.at[g])
        if tiles > 1:
            grad[...] = jnp.zeros_like(grad)

        def one_tile(t, inner_carry):
            lanes = pl.ds(pl.multiple_of(t * width, width), width)
            info = met[g, :, lanes].astype(jnp.float32)
            lat_w = weight_rows(info[0:1], info[2:3], pad)
            lon_w = weight_rows(info[1:2], info[3:4], pad)
            lon_c = lon_w[:cols]
            lon_e = lon_w[cols:cols + 1]
            lat_n_row = lat_w[rows:rows + 1] * inside
            first = lax.broadcasted_iota(jnp.int32, (rows, width), 0) == 0
            blocks = [lat_w[r:r + 1] * lon_c for r in range(rows)]
            blocks.append(lat_n_row * lon_c)
            blocks.append(lat_w[:rows] * lon_e)
            blocks.append(
                jnp.where(first, jnp.broadcast_to(lat_n_row * lon_e, (rows, width)), 0.0)
            )
            spread = jnp.concatenate(blocks, axis=0).astype(jnp.bfloat16).astype(jnp.float32)
            jac_t = jrecv[g, lanes]
            products = lax.dot_general(
                tbl[g], jac_t, (((1,), (1,)), ((), ())), preferred_element_type=jnp.float32
            )
            evolved = jnp.sum(spread * products, axis=0, keepdims=True)
            departure = jnp.where(info[0:1] >= 0.0, evolved - info[4:5], 0.0)
            dep[g, :, lanes] = departure
            scaled = (spread * (info[5:6] * departure)).astype(jnp.bfloat16)
            partial = jnp.dot(scaled, jac_t, preferred_element_type=jnp.float32)
            if tiles > 1:
                grad[...] += partial
            else:
                grad[...] = partial
            return inner_carry

        if tiles > 1:
            lax.fori_loop(0, tiles, one_tile, 0)
        else:
            one_tile(0, 0)
        gsend[g] = grad[...].astype(jnp.bfloat16)
        east = (g * inner + xi + 1) % lon_n
        remote(gsend.at[g, pl.ds(cells, cols)], hrecv.at[0, z], h_send, h_recv,
               (lat_up, g * inner + xi)).start()
        remote(gsend.at[g, pl.ds(halo, rows)], hrecv.at[1, z], h_send, h_recv,
               (lat, east)).start()
        remote(gsend.at[g, pl.ds(halo + rows, rows)], hrecv.at[2, z], h_send, h_recv,
               (lat_up, east)).start()

        @pl.when(n < line - 1)
        def _():
            slot = (g - z - 1 + line) % line
            remote(gsend.at[g, pl.ds(0, cells)], grecv.at[slot], g_send, g_recv,
                   (lat, g * inner + xi)).start()

        def send_dep(i, inner_carry):
            to = (here + i) % plane
            remote(
                dep.at[g, :, pl.ds(to * slots, slots)], dep_out.at[lat, g, xi], d_send, d_recv,
                (to // inner, z * inner + to % inner),
            ).start()
            return inner_carry

        lax.fori_loop(1, plane, send_dep, 0)
        pltpu.make_async_copy(dep.at[g, :, mine], dep_out.at[lat, g, xi], d_recv).start()
        return carry

    lax.fori_loop(0, line, group, 0)

    others = pl.ds(0, (plane - 1) * slots)
    landed(grecv, g_recv)
    landed(hrecv, h_recv)
    landed(dep_out, d_recv)
    landed(tbl.at[0, pl.ds(cells, cols + 2 * rows)], e_send)
    for slot in range(line):
        @pl.when(jnp.logical_and(has_high, z >= slot))
        def _():
            landed(tbl.at[slot], t_send.at[0, slot])

        @pl.when(jnp.logical_and(has_low, z <= slot))
        def _():
            landed(tbl.at[slot], t_send.at[1, slot])

    landed(met.at[:, :, others], m_send)
    landed(jrecv.at[:, others], j_send)
    landed(dep.at[:, :, others], d_send)
    landed(grecv, g_send)
    landed(gsend.at[:, pl.ds(cells, cols + 2 * rows)], h_send)


def last_sums(rows, cols, grad, grecv, hrecv, dep, grad_out, dep_out):
    dep_out[...] = dep[...]
    field_sum = grad[pl.ds(0, rows * cols), :]
    for slot in range(grecv.shape[0]):
        field_sum = field_sum + grecv[slot].astype(jnp.float32)
    grad_out[...] = field_sum
    grad_out[pl.ds(0, cols), :] += jnp.sum(hrecv[0].astype(jnp.float32), axis=0)
    east_sum = jnp.sum(hrecv[1].astype(jnp.float32), axis=0)
    corner_sum = jnp.sum(hrecv[2].astype(jnp.float32), axis=0)
    for r in range(rows):
        extra = east_sum[r:r + 1]
        if r == 0:
            extra = extra + corner_sum[0:1]
        grad_out[pl.ds(r * cols, 1), :] += extra


def shards(mesh_shape, field, obs_jac, obs_frac, obs_innov, obs_rinv, obs_cells):
    lat_n, lon_n = mesh_shape
    line = math.gcd(lon_n // 2, 4)
    inner = lon_n // line
    plane = lat_n * inner
    total = lat_n * lon_n
    rows, cols, wide = field.shape
    slots = obs_jac.shape[2]
    tile = math.gcd(plane, 8)
    cells = rows * cols
    table = cells + cols + 2 * rows
    f32, bf16 = jnp.float32, jnp.bfloat16
    dma = pltpu.SemaphoreType.DMA
    one = pltpu.SemaphoreType.DMA(())
    vmem = pl.BlockSpec(memory_space=pltpu.VMEM)
    parts = pl.pallas_call(
        functools.partial(kernel, lat_n, lon_n, line, rows, cols, tile),
        out_shape=(
            jax.ShapeDtypeStruct((table, wide), f32),
            jax.ShapeDtypeStruct((line - 1, cells, wide), bf16),
            jax.ShapeDtypeStruct((3, line, rows, wide), bf16),
            jax.ShapeDtypeStruct((lat_n, line, inner, 1, slots), f32),
        ),
        in_specs=[vmem, vmem, vmem, vmem, vmem, pl.BlockSpec(memory_space=pl.ANY)],
        out_specs=(vmem,) * 4,
        scratch_shapes=[
            pltpu.VMEM((rows, wide), bf16),
            pltpu.VMEM((total, slots), f32),
            pltpu.VMEM((total, slots), f32),
            pltpu.VMEM((plane, line, 8, slots), bf16),
            pltpu.VMEM((line, table, wide), bf16),
            pltpu.VMEM((line, 8, plane * slots), bf16),
            pltpu.VMEM((line, plane * slots, wide), bf16),
            pltpu.VMEM((line, 1, plane * slots), f32),
            pltpu.VMEM((line, table, wide), bf16),
            one, dma((2, line)), dma((line,)),
            one, one,
            one, dma((line,)),
            one, one,
            one, one,
            one, one,
            pltpu.SemaphoreType.REGULAR, pltpu.SemaphoreType.REGULAR,
        ],
        compiler_params=pltpu.CompilerParams(
            collective_id=0, has_side_effects=True, vmem_limit_bytes=60 * 1024 * 1024
        ),
    )(
        field.reshape(cells, wide),
        obs_cells,
        obs_frac.reshape(total, 2, slots),
        obs_innov.reshape(total, slots),
        obs_rinv.reshape(total, slots),
        obs_jac.reshape(lat_n, line, inner, slots, wide),
    )
    grad, departures = pl.pallas_call(
        functools.partial(last_sums, rows, cols),
        out_shape=(
            jax.ShapeDtypeStruct((cells, wide), f32),
            jax.ShapeDtypeStruct((total, 1, slots), f32),
        ),
        in_specs=[vmem] * 4,
        out_specs=(vmem, vmem),
    )(*parts[:3], parts[3].reshape(total, 1, slots))
    return departures, grad.reshape(rows, cols, wide)


def solution(mesh):
    placed = (
        P("lat", "lon", None),
        P(None, ("lat", "lon"), None, None),
        P(None, ("lat", "lon"), None, None),
        P(None, ("lat", "lon"), None),
        P(None, ("lat", "lon"), None),
        P(None, ("lat", "lon"), None),
    )
    return jax.shard_map(
        functools.partial(shards, (mesh.shape["lat"], mesh.shape["lon"])),
        mesh=mesh,
        in_specs=placed,
        out_specs=(P(None, ("lat", "lon"), None), P("lat", "lon", None)),
        check_vma=False,
    )
```

```python
import functools
import math

import jax
import jax.numpy as jnp
from jax import lax
from jax.experimental import pallas as pl
from jax.experimental.pallas import tpu as pltpu
from jax.sharding import PartitionSpec as P

MESH = pl.DeviceIdType.MESH
AWAY = -1000.0


def weight_rows(position, frac, rows):
    ids = lax.broadcasted_iota(jnp.int32, (rows, position.shape[1]), 0).astype(jnp.float32)
    zero = jnp.zeros_like(ids)
    return jnp.where(
        ids == position, 1.0 - frac, jnp.where(ids == position + 1.0, frac, zero)
    )


def kernel(
    lat_n, lon_n, line, rows, cols, tile,
    field, cell_ref, frac_ref, innov_ref, rinv_ref, jac,
    grad, grecv, hrecv, dep_out,
    edge, innov, rinv, meta,
    tbl, met, jrecv, dep, gsend,
    t_send, t_recv, m_send, m_recv, j_send, j_recv, d_send, d_recv,
    g_send, g_recv, h_send, h_recv, from_low, from_high,
):
    inner = lon_n // line
    plane = lat_n * inner
    total = lat_n * lon_n
    slots = jac.shape[3]
    cells = rows * cols
    halo = cells + cols
    lat, lon = lax.axis_index("lat"), lax.axis_index("lon")
    z, xi = lon // inner, lon % inner
    here = lat * inner + xi
    lat_up, lat_down = (lat + 1) % lat_n, (lat + lat_n - 1) % lat_n
    lon_down = (lon + lon_n - 1) % lon_n
    z_low, x_low = lon_down // inner, lon_down % inner

    def remote(src, dst, send, recv, to):
        return pltpu.make_async_remote_copy(
            src_ref=src, dst_ref=dst, send_sem=send, recv_sem=recv,
            device_id=to, device_id_type=MESH,
        )

    def landed(like, sem):
        pltpu.make_async_copy(like, like, sem).wait()

    has_low, has_high = z > 0, z < line - 1
    low, high = (lat, lon - inner), (lat, lon + inner)
    barrier = pltpu.get_barrier_semaphore()

    @pl.when(has_low)
    def _():
        pl.semaphore_signal(barrier, inc=1, device_id=low, device_id_type=MESH)

    @pl.when(has_high)
    def _():
        pl.semaphore_signal(barrier, inc=1, device_id=high, device_id_type=MESH)

    def greet(i, carry):
        to = (here + i) % plane
        pl.semaphore_signal(
            barrier, inc=1, device_id=(to // inner, z * inner + to % inner), device_id_type=MESH
        )
        return carry

    lax.fori_loop(1, plane, greet, 0)

    mine = pl.ds(here * slots, slots)
    pltpu.make_async_copy(field, tbl.at[z, pl.ds(0, cells)], t_recv.at[z]).start()
    for n in range(line):
        g = (z + 1 + n) % line
        pltpu.make_async_copy(jac.at[lat, g, xi], jrecv.at[g, mine], j_recv.at[g]).start()
    pl.semaphore_wait(barrier, plane - 1 + has_low.astype(jnp.int32) + has_high.astype(jnp.int32))

    def send_jac(g):
        def one(i, carry):
            to = (here + i) % plane
            remote(
                jac.at[to // inner, g, to % inner], jrecv.at[g, mine], j_send, j_recv.at[g],
                (to // inner, z * inner + to % inner),
            ).start()
            return carry

        lax.fori_loop(1, plane, one, 0)

    def send_meta(i, carry):
        to = (here + i) % plane
        remote(
            meta.at[to], met.at[:, :, mine], m_send, m_recv,
            (to // inner, z * inner + to % inner),
        ).start()
        return carry

    send_jac((z + 1) % line)
    edge[...] = jnp.concatenate(
        [field[pl.ds(r * cols, cols), :].astype(jnp.float32)[0:1] for r in range(rows)], axis=0
    ).astype(edge.dtype)

    for _ in range(line - 1):
        @pl.when(has_low)
        def _():
            pl.semaphore_signal(from_high, inc=1, device_id=low, device_id_type=MESH)

        @pl.when(has_high)
        def _():
            pl.semaphore_signal(from_low, inc=1, device_id=high, device_id_type=MESH)

        @pl.when(has_low)
        def _():
            pl.semaphore_wait(from_low, 1)

        @pl.when(has_high)
        def _():
            pl.semaphore_wait(from_high, 1)

    for i in (*range(1, line), 0):
        to = (z + i) % line
        if i > 0:
            remote(field, tbl.at[z, pl.ds(0, cells)], t_send.at[0], t_recv.at[z],
                   (lat, to * inner + xi)).start()
        remote(field.at[pl.ds(0, cols)], tbl.at[z, pl.ds(cells, cols)], t_send.at[1],
               t_recv.at[z], (lat_down, to * inner + xi)).start()
        remote(edge, tbl.at[z_low, pl.ds(halo, rows)], t_send.at[1], t_recv.at[z_low],
               (lat, to * inner + x_low)).start()
        remote(edge, tbl.at[z_low, pl.ds(halo + rows, rows)], t_send.at[1], t_recv.at[z_low],
               (lat_down, to * inner + x_low)).start()
    send_jac((z + 2) % line)
    innov[...] = innov_ref[...].astype(jnp.float32)
    rinv[...] = rinv_ref[...].astype(jnp.float32)

    def build(k, carry):
        for g in range(line):
            owner = (k // inner) * lon_n + g * inner + k % inner
            cell = cell_ref[owner].astype(jnp.float32)
            live = cell >= 0.0
            row = jnp.floor((cell + 0.5) * (1.0 / (cols + 1)))
            meta[k, g] = jnp.concatenate(
                [
                    jnp.where(live, row, AWAY),
                    jnp.where(live, cell - row * (cols + 1), AWAY),
                    frac_ref[owner].astype(jnp.float32),
                    innov[pl.ds(owner, 1), :],
                    rinv[pl.ds(owner, 1), :],
                    jnp.zeros((2, slots), jnp.float32),
                ],
                axis=0,
            ).astype(meta.dtype)
        return carry

    lax.fori_loop(0, plane, build, 0)
    pltpu.make_async_copy(meta.at[here], met.at[:, :, mine], m_recv).start()

    lax.fori_loop(1, plane, send_meta, 0)
    for n in range(2, line):
        send_jac((z + 1 + n) % line)

    landed(met, m_recv)
    inside = jnp.where(lat < lat_n - 1, 1.0, 0.0)
    width = tile * slots
    tiles = plane // tile
    pad = -(-(max(rows, cols) + 1) // 8) * 8

    def group(n, carry):
        g = (z + 1 + n) % line
        landed(tbl.at[g], t_recv.at[g])
        landed(jrecv.at[g], j_recv.at[g])
        if tiles > 1:
            grad[...] = jnp.zeros_like(grad)

        def one_tile(t, inner_carry):
            lanes = pl.ds(pl.multiple_of(t * width, width), width)
            info = met[g, :, lanes].astype(jnp.float32)
            lat_w = weight_rows(info[0:1], info[2:3], pad)
            lon_w = weight_rows(info[1:2], info[3:4], pad)
            lon_c = lon_w[:cols]
            lon_e = lon_w[cols:cols + 1]
            lat_n_row = lat_w[rows:rows + 1] * inside
            first = lax.broadcasted_iota(jnp.int32, (rows, width), 0) == 0
            blocks = [lat_w[r:r + 1] * lon_c for r in range(rows)]
            blocks.append(lat_n_row * lon_c)
            blocks.append(lat_w[:rows] * lon_e)
            blocks.append(
                jnp.where(first, jnp.broadcast_to(lat_n_row * lon_e, (rows, width)), 0.0)
            )
            spread = jnp.concatenate(blocks, axis=0).astype(jnp.bfloat16).astype(jnp.float32)
            jac_t = jrecv[g, lanes]
            products = lax.dot_general(
                tbl[g], jac_t, (((1,), (1,)), ((), ())), preferred_element_type=jnp.float32
            )
            evolved = jnp.sum(spread * products, axis=0, keepdims=True)
            departure = jnp.where(info[0:1] >= 0.0, evolved - info[4:5], 0.0)
            dep[g, :, lanes] = departure
            scaled = (spread * (info[5:6] * departure)).astype(jnp.bfloat16)
            partial = jnp.dot(scaled, jac_t, preferred_element_type=jnp.float32)
            if tiles > 1:
                grad[...] += partial
            else:
                grad[...] = partial
            return inner_carry

        if tiles > 1:
            lax.fori_loop(0, tiles, one_tile, 0)
        else:
            one_tile(0, 0)
        gsend[g] = grad[...].astype(jnp.bfloat16)
        east = (g * inner + xi + 1) % lon_n
        remote(gsend.at[g, pl.ds(cells, cols)], hrecv.at[0, z], h_send, h_recv,
               (lat_up, g * inner + xi)).start()
        remote(gsend.at[g, pl.ds(halo, rows)], hrecv.at[1, z], h_send, h_recv,
               (lat, east)).start()
        remote(gsend.at[g, pl.ds(halo + rows, rows)], hrecv.at[2, z], h_send, h_recv,
               (lat_up, east)).start()

        @pl.when(n < line - 1)
        def _():
            slot = lax.rem(n, line - 1)
            remote(gsend.at[g, pl.ds(0, cells)], grecv.at[slot], g_send, g_recv,
                   (lat, g * inner + xi)).start()

        def send_dep(i, inner_carry):
            to = (here + i) % plane
            remote(
                dep.at[g, :, pl.ds(to * slots, slots)], dep_out.at[lat, g, xi], d_send, d_recv,
                (to // inner, z * inner + to % inner),
            ).start()
            return inner_carry

        lax.fori_loop(1, plane, send_dep, 0)
        pltpu.make_async_copy(dep.at[g, :, mine], dep_out.at[lat, g, xi], d_recv).start()
        return carry

    lax.fori_loop(0, line, group, 0)

    others = pl.ds(0, (plane - 1) * slots)
    landed(grecv, g_recv)
    landed(hrecv, h_recv)
    landed(dep_out, d_recv)
    landed(grecv, t_send.at[0])
    landed(tbl.at[:, pl.ds(cells, cols + 2 * rows)], t_send.at[1])
    landed(met.at[:, :, others], m_send)
    landed(jrecv.at[:, others], j_send)
    landed(dep.at[:, :, others], d_send)
    landed(grecv, g_send)
    landed(gsend.at[:, pl.ds(cells, cols + 2 * rows)], h_send)


def last_sums(rows, cols, grad, grecv, hrecv, dep, grad_out, dep_out):
    dep_out[...] = dep[...]
    field_sum = grad[pl.ds(0, rows * cols), :]
    for slot in range(grecv.shape[0]):
        field_sum = field_sum + grecv[slot].astype(jnp.float32)
    grad_out[...] = field_sum
    grad_out[pl.ds(0, cols), :] += jnp.sum(hrecv[0].astype(jnp.float32), axis=0)
    east_sum = jnp.sum(hrecv[1].astype(jnp.float32), axis=0)
    corner_sum = jnp.sum(hrecv[2].astype(jnp.float32), axis=0)
    for r in range(rows):
        extra = east_sum[r:r + 1]
        if r == 0:
            extra = extra + corner_sum[0:1]
        grad_out[pl.ds(r * cols, 1), :] += extra


def shards(mesh_shape, field, obs_jac, obs_frac, obs_innov, obs_rinv, obs_cells):
    lat_n, lon_n = mesh_shape
    line = math.gcd(lon_n // 2, 4)
    inner = lon_n // line
    plane = lat_n * inner
    total = lat_n * lon_n
    rows, cols, wide = field.shape
    slots = obs_jac.shape[2]
    tile = math.gcd(plane, 8)
    cells = rows * cols
    table = cells + cols + 2 * rows
    f32, bf16 = jnp.float32, jnp.bfloat16
    dma = pltpu.SemaphoreType.DMA
    one = pltpu.SemaphoreType.DMA(())
    vmem = pl.BlockSpec(memory_space=pltpu.VMEM)
    parts = pl.pallas_call(
        functools.partial(kernel, lat_n, lon_n, line, rows, cols, tile),
        out_shape=(
            jax.ShapeDtypeStruct((table, wide), f32),
            jax.ShapeDtypeStruct((line - 1, cells, wide), bf16),
            jax.ShapeDtypeStruct((3, line, rows, wide), bf16),
            jax.ShapeDtypeStruct((lat_n, line, inner, 1, slots), f32),
        ),
        in_specs=[vmem, vmem, vmem, vmem, vmem, pl.BlockSpec(memory_space=pl.ANY)],
        out_specs=(vmem,) * 4,
        scratch_shapes=[
            pltpu.VMEM((rows, wide), bf16),
            pltpu.VMEM((total, slots), f32),
            pltpu.VMEM((total, slots), f32),
            pltpu.VMEM((plane, line, 8, slots), bf16),
            pltpu.VMEM((line, table, wide), bf16),
            pltpu.VMEM((line, 8, plane * slots), bf16),
            pltpu.VMEM((line, plane * slots, wide), bf16),
            pltpu.VMEM((line, 1, plane * slots), f32),
            pltpu.VMEM((line, table, wide), bf16),
            dma((2,)), dma((line,)),
            one, one,
            one, dma((line,)),
            one, one,
            one, one,
            one, one,
            pltpu.SemaphoreType.REGULAR, pltpu.SemaphoreType.REGULAR,
        ],
        compiler_params=pltpu.CompilerParams(
            collective_id=0, has_side_effects=True, vmem_limit_bytes=60 * 1024 * 1024
        ),
    )(
        field.reshape(cells, wide),
        obs_cells,
        obs_frac.reshape(total, 2, slots),
        obs_innov.reshape(total, slots),
        obs_rinv.reshape(total, slots),
        obs_jac.reshape(lat_n, line, inner, slots, wide),
    )
    grad, departures = pl.pallas_call(
        functools.partial(last_sums, rows, cols),
        out_shape=(
            jax.ShapeDtypeStruct((cells, wide), f32),
            jax.ShapeDtypeStruct((total, 1, slots), f32),
        ),
        in_specs=[vmem] * 4,
        out_specs=(vmem, vmem),
    )(*parts[:3], parts[3].reshape(total, 1, slots))
    return departures, grad.reshape(rows, cols, wide)


def solution(mesh):
    placed = (
        P("lat", "lon", None),
        P(None, ("lat", "lon"), None, None),
        P(None, ("lat", "lon"), None, None),
        P(None, ("lat", "lon"), None),
        P(None, ("lat", "lon"), None),
        P(None, ("lat", "lon"), None),
    )
    return jax.shard_map(
        functools.partial(shards, (mesh.shape["lat"], mesh.shape["lon"])),
        mesh=mesh,
        in_specs=placed,
        out_specs=(P(None, ("lat", "lon"), None), P("lat", "lon", None)),
        check_vma=False,
    )
```
